32 devices in a mesh: tm: 4 (over x, core), tile: 8 (over z, y).
Axes of the slice: x: 2, y: 2, z: 4, core: 2. Of those that a mesh axis runs over, the one named last changes fastest.
Arguments:
- pcs: float32 [2, 256], P(None, 'tm'), may hold values from -6 to 6
- st_eof: float32 [2, 120, 512], replicated, may hold values from -6 to 6
- spatial_eof: bfloat16 [2, 512, 64, 2048], P(None, 'tm', 'tile'), may hold values from -1 to 1
- land_sea: int32 [64, 2048], P('tile'), may hold values 0 or 1
Outputs:
- vorticity: float32 [256, 64, 2048], P('tm', 'tile')
- divergence: float32 [256, 64, 2048], P('tm', 'tile')
The draws below stay inside these ranges and needn't reach their ends.
All inputs are finite; a program needn't handle non-finite values. No bound on the sum of `land_sea` on one device may be relied on, other than what follows from the above.
Results may differ from the reference program's by a relative error of at most 0.0041.
Values may be sent and summed in bfloat16 or wider, within the bound.
A program may use at most 128 MiB of HBM per device.

```python
import math
import jax
import jax.numpy as jnp
from jax import lax

C = 512
M = 120
K = 2
NLON = 2048
DAYS = 256
NLAT = 64


def with_ends(array, key, low, high):
    extent = array.shape
    place = [jax.random.randint(jax.random.fold_in(key, axis), (), 0, extent[axis]) for axis in range(len(extent))]
    array = array.at[tuple(place)].set(low)
    longest = extent.index(max(extent))
    place[longest] = (place[longest] + 1) % extent[longest]
    return array.at[tuple(place)].set(high)


def levels(rng, shape, pieces, least, high):
    loudness = 1.0
    for axis_at, shards_of in pieces:
        heights = jax.random.uniform(jax.random.fold_in(jax.random.fold_in(rng, 6), axis_at), (shards_of,), jnp.float32, least / len(pieces), high / len(pieces))
        loudness = loudness * jnp.repeat(jnp.exp(heights), shape[axis_at] // shards_of).reshape((-1,) + (1,) * (len(shape) - 1 - axis_at))
    return loudness


def gaussian(stream_key, dims, width, reach, pieces=(), held_as=jnp.bfloat16):
    entries = width * jax.random.normal(stream_key, dims, jnp.float32)
    if pieces:
        entries = entries * levels(stream_key, dims, pieces, -0.22, 0.18)
    return jnp.clip(entries, -reach, reach).astype(held_as)


def setup_inputs(seed: int = 0) -> dict:
    key_list = jax.random.split(jax.random.key(seed), 5)
    return {
        "pcs": gaussian(key_list[0], (K, DAYS), 1.0, 6.0, ((1, 4),), jnp.float32),
        "st_eof": gaussian(key_list[1], (K, M, C), 1.0, 6.0, (), jnp.float32),
        "spatial_eof": gaussian(key_list[2], (2, C, NLAT, NLON), (C // 16) ** -0.5, 1.0, ((1, 4), (2, 8))),
        "land_sea": with_ends((jax.random.randint(key_list[3], (NLAT, NLON), 0, 4) < 3).astype(jnp.int32), jax.random.fold_in(key_list[3], 1), 0, 1),
    }


def lagged_rc(series, st_eof, first, count):
    day_index = first + jnp.arange(count, dtype=jnp.int32)
    lag_steps = jnp.arange(M, dtype=jnp.int32)
    lag_index = day_index[:, None] - lag_steps[None, :]
    inside = lag_index >= 0
    safe_index = jnp.maximum(lag_index, 0)
    values_lag = jnp.where(inside[None], series[:, safe_index], 0.0)
    lagged = jnp.transpose(values_lag, (1, 0, 2)).reshape(count, K * M)
    lagged_sums = jnp.dot(lagged, st_eof.reshape(K * M, -1), precision=lax.Precision.HIGHEST, preferred_element_type=jnp.float32)
    window_len = jnp.minimum(day_index + 1, M).astype(lagged_sums.dtype)
    return lagged_sums / window_len[:, None]


def curl_div(east_pad, north_pad, latitude):
    cosine = jnp.cos(latitude)
    cos_east = east_pad * cosine[None, :, None]
    cos_north = north_pad * cosine[None, :, None]
    inner_east = east_pad[:, 1:-1]
    inner_north = north_pad[:, 1:-1]
    zonal_east = jnp.roll(inner_east, -1, axis=2) - jnp.roll(inner_east, 1, axis=2)
    zonal_north = jnp.roll(inner_north, -1, axis=2) - jnp.roll(inner_north, 1, axis=2)
    denominator = 2.0 * cosine[1:-1][None, :, None]
    vorticity = (zonal_north - (cos_east[:, 2:] - cos_east[:, :-2])) / denominator
    divergence = (zonal_east + (cos_north[:, 2:] - cos_north[:, :-2])) / denominator
    return vorticity, divergence


def reference(pcs, st_eof, spatial_eof, land_sea):
    components = lagged_rc(pcs, st_eof, 0, DAYS).astype(jnp.bfloat16)
    cell_count = NLAT * NLON
    ocean_mask = land_sea.astype(jnp.float32)
    east_vel = jnp.dot(components, spatial_eof[0].reshape(C, cell_count), preferred_element_type=jnp.float32).reshape(DAYS, NLAT, NLON)
    north_vel = jnp.dot(components, spatial_eof[1].reshape(C, cell_count), preferred_element_type=jnp.float32).reshape(DAYS, NLAT, NLON)
    east_vel = (east_vel * ocean_mask[None]).astype(jnp.bfloat16).astype(jnp.float32)
    north_vel = (north_vel * ocean_mask[None]).astype(jnp.bfloat16).astype(jnp.float32)
    east_pad = jnp.pad(east_vel, ((0, 0), (1, 1), (0, 0)))
    north_pad = jnp.pad(north_vel, ((0, 0), (1, 1), (0, 0)))
    global_rows = jnp.arange(-1, NLAT + 1, dtype=jnp.float32)
    latitude = (-70.0 + 140.0 * (global_rows + 0.5) / NLAT) * (math.pi / 180.0)
    vorticity, divergence = curl_div(east_pad, north_pad, latitude)
    return vorticity * ocean_mask[None], divergence * ocean_mask[None]
```

```python
import functools
import math

import jax
import jax.numpy as jnp
from jax import lax
from jax.experimental import pallas as pl
from jax.experimental.pallas import tpu as pltpu
from jax.sharding import PartitionSpec as P

MESH = pl.DeviceIdType.MESH
F32 = jnp.float32
BF16 = jnp.bfloat16


def iota(shape, axis):
    return lax.broadcasted_iota(jnp.int32, shape, axis)


def kernel(
    dims,
    pcs_ref,
    st_ref,
    eof_ref,
    mask_ref,
    coef_ref,
    vort_ref,
    div_ref,
    pcs_slots,
    st_buf,
    eof_buf,
    mix,
    send_buf,
    recv_buf,
    vel,
    halo_send,
    halo_recv,
    out_buf,
    st_sem,
    pcs_ssem,
    pcs_rsem,
    eof_lsem,
    eof_ssem,
    eof_rsem,
    part_ssem,
    part_rsem,
    halo_ssem,
    halo_rsem,
    out_sem,
):
    n_tm, n_tile, days, lat, width, chunks, lags, chan = dims
    rows = days * lat
    depth = chan * lat
    me = lax.axis_index("tm")
    tile = lax.axis_index("tile")
    partner = me + 1 - 2 * lax.rem(me, 2)
    cross = lax.rem(me + n_tm // 2, n_tm)
    has_low = tile > 0
    has_high = tile < n_tile - 1

    st_copy = pltpu.make_async_copy(st_ref, st_buf.at[:, pl.ds(0, lags)], st_sem)
    st_copy.start()

    def eof_local(n):
        src = eof_ref.at[:, :, pl.ds(pl.multiple_of(n * width, width), width)]
        return pltpu.make_async_copy(src, eof_buf.at[n, :, pl.ds(0, depth)], eof_lsem.at[n])

    def eof_remote(n):
        src = eof_ref.at[:, :, pl.ds(pl.multiple_of(n * width, width), width)]
        return pltpu.make_async_remote_copy(
            src_ref=src,
            dst_ref=eof_buf.at[n, :, pl.ds(depth, depth)],
            send_sem=eof_ssem.at[n],
            recv_sem=eof_rsem.at[n],
            device_id=(partner, tile),
            device_id_type=MESH,
        )

    def part_copy(n):
        return pltpu.make_async_remote_copy(
            src_ref=send_buf.at[n],
            dst_ref=recv_buf.at[n],
            send_sem=part_ssem.at[n],
            recv_sem=part_rsem.at[n],
            device_id=(cross, tile),
            device_id_type=MESH,
        )

    def halo_down(n):
        return pltpu.make_async_remote_copy(
            src_ref=halo_send.at[n, :, pl.ds(0, days)],
            dst_ref=halo_recv.at[n, :, pl.ds(days, days)],
            send_sem=halo_ssem.at[0, n],
            recv_sem=halo_rsem.at[0, n],
            device_id=(me, tile - 1),
            device_id_type=MESH,
        )

    def halo_up(n):
        return pltpu.make_async_remote_copy(
            src_ref=halo_send.at[n, :, pl.ds(days, days)],
            dst_ref=halo_recv.at[n, :, pl.ds(0, days)],
            send_sem=halo_ssem.at[1, n],
            recv_sem=halo_rsem.at[1, n],
            device_id=(me, tile + 1),
            device_id_type=MESH,
        )

    def out_copies(n):
        cols = pl.ds(pl.multiple_of(n * width, width), width)
        return [
            pltpu.make_async_copy(out_buf.at[n, q], ref.at[:, cols], out_sem.at[q, n])
            for q, ref in enumerate((vort_ref, div_ref))
        ]

    lax.fori_loop(0, chunks, lambda n, c: (eof_local(n).start(), c)[1], 0)

    barrier = pltpu.get_barrier_semaphore()
    for step in range(1, n_tm):
        pl.semaphore_signal(
            barrier, inc=1, device_id=(lax.rem(me + step, n_tm), tile), device_id_type=MESH
        )

    @pl.when(has_low)
    def _():
        pl.semaphore_signal(barrier, inc=1, device_id=(me, tile - 1), device_id_type=MESH)

    @pl.when(has_high)
    def _():
        pl.semaphore_signal(barrier, inc=1, device_id=(me, tile + 1), device_id_type=MESH)

    neighbours = has_low.astype(jnp.int32) + has_high.astype(jnp.int32)
    pl.semaphore_wait(barrier, n_tm - 1 + neighbours)

    pcs_copies = []
    for step in range(1, n_tm):
        copy = pltpu.make_async_remote_copy(
            src_ref=pcs_ref,
            dst_ref=pcs_slots.at[step - 1],
            send_sem=pcs_ssem.at[step - 1],
            recv_sem=pcs_rsem.at[step - 1],
            device_id=(lax.rem(me + step, n_tm), tile),
            device_id_type=MESH,
        )
        copy.start()
        pcs_copies.append(copy)
    lax.fori_loop(0, chunks, lambda n, c: (eof_remote(n).start(), c)[1], 0)

    lag_pad = st_buf.shape[1]
    if lag_pad > lags:
        st_buf[:, lags:] = jnp.zeros((st_buf.shape[0], lag_pad - lags, st_buf.shape[2]), F32)

    @pl.when(jnp.logical_not(has_low))
    def _():
        halo_recv[:, :, pl.ds(0, days)] = jnp.zeros((chunks, 2, days, width), BF16)

    @pl.when(jnp.logical_not(has_high))
    def _():
        halo_recv[:, :, pl.ds(days, days)] = jnp.zeros((chunks, 2, days, width), BF16)

    st_copy.wait()
    backward = pcs_ref[...]
    for copy in pcs_copies:
        copy.wait()
    for step in range(1, n_tm):
        backward = backward + pcs_slots[step - 1]
    total_days = backward.shape[1]

    repeat_rows = (
        (iota((rows, days), 0) >= iota((rows, days), 1) * lat)
        & (iota((rows, days), 0) < iota((rows, days), 1) * lat + lat)
    ).astype(BF16)
    piece = 2 * 128
    for slot, target in enumerate((cross, me)):
        first = target * days
        day = first + iota((days, lag_pad), 0)
        lag = iota((days, lag_pad), 1)
        inside = (lag <= day) & (lag < lags)
        lagged = []
        for k in range(st_buf.shape[0]):
            wide = jnp.broadcast_to(backward[k : k + 1], (days, total_days))
            wide = pltpu.roll(wide, first + 1, 1)
            at = iota((days, total_days), 0)
            bit = 1
            while bit < days:
                wide = jnp.where((at & bit) != 0, pltpu.roll(wide, bit, 1), wide)
                bit *= 2
            lagged.append(jnp.where(inside, wide[:, :lag_pad], 0.0))
        window = jnp.minimum(first + iota((days, chan), 0) + 1, lags).astype(F32)
        for part, owner in enumerate((me, partner)):
            cols = pl.ds(pl.multiple_of(owner * chan, chan), chan)
            sums = jnp.zeros((days, chan), F32)
            for k in range(st_buf.shape[0]):
                sums = sums + jnp.dot(
                    lagged[k],
                    st_buf[k, :, cols],
                    precision=lax.Precision.HIGHEST,
                    preferred_element_type=F32,
                )
            comp = (sums / window).astype(BF16)
            tall = jnp.dot(repeat_rows, comp, preferred_element_type=F32).astype(BF16)
            for start in range(0, depth, piece):
                c_at = iota((chan, piece), 0) * lat
                col_at = iota((chan, piece), 1) + start
                expand = ((col_at >= c_at) & (col_at < c_at + lat)).astype(BF16)
                spread = jnp.dot(tall, expand, preferred_element_type=F32)
                same = (iota((rows, piece), 0) & (lat - 1)) == (iota((rows, piece), 1) & (lat - 1))
                mix[slot, :, part * depth + start : part * depth + start + piece] = jnp.where(
                    same, spread, 0.0
                ).astype(BF16)

    def send_part(n, carry):
        eof_local(n).wait()
        eof_remote(n).wait_recv()
        for x in range(2):
            send_buf[n, x] = jnp.dot(
                mix[0], eof_buf[n, x], preferred_element_type=F32
            ).astype(BF16)
        part_copy(n).start()
        return carry

    lax.fori_loop(0, chunks, send_part, 0)

    edge = iota((2 * days, rows), 0)
    row = iota((2 * days, rows), 1)
    pick = ((edge < days) & (row == edge * lat)) | (
        (edge >= days) & (row == (edge - days) * lat + lat - 1)
    )
    edge_t = iota((rows, 2 * days), 1)
    row_t = iota((rows, 2 * days), 0)
    place = ((edge_t < days) & (row_t == edge_t * lat)) | (
        (edge_t >= days) & (row_t == (edge_t - days) * lat + lat - 1)
    )
    pick = pick.astype(BF16)
    place = place.astype(BF16)

    def make_velocity(n):
        own = [jnp.dot(mix[1], eof_buf[n, x], preferred_element_type=F32) for x in range(2)]
        part_copy(n).wait_recv()
        ocean = mask_ref[:, pl.ds(pl.multiple_of(n * width, width), width)].astype(F32)
        for x in range(2):
            total = (own[x] + recv_buf[n, x].astype(F32)).reshape(days, lat, width)
            vel[n, x] = (total * ocean[None]).reshape(rows, width).astype(BF16)
        for x in range(2):
            halo_send[n, x] = jnp.dot(pick, vel[n, x], preferred_element_type=F32).astype(BF16)

        @pl.when(has_low)
        def _():
            halo_down(n).start()

        @pl.when(has_high)
        def _():
            halo_up(n).start()

    def stencil(n):
        before = lax.rem(n + chunks - 1, chunks)
        after = lax.rem(n + 1, chunks)

        @pl.when(has_low)
        def _():
            halo_up(n).wait_recv()

        @pl.when(has_high)
        def _():
            halo_down(n).wait_recv()

        shape = (days, lat, width)
        lane = iota((lat, width), 1)[None]
        line = iota((lat, width), 0)[None]
        cosine = coef_ref[0:lat][None]
        outer = coef_ref[lat : 2 * lat][None]
        ocean = mask_ref[:, pl.ds(pl.multiple_of(n * width, width), width)].astype(F32)
        scale = (ocean * coef_ref[2 * lat : 3 * lat])[None]
        zonal = []
        meridional = []
        for x in range(2):
            here = vel[n, x].astype(F32).reshape(rows, width)
            west = vel[before, x].astype(F32)
            east = vel[after, x].astype(F32)
            up = jnp.where(
                lane == width - 1,
                pltpu.roll(east, width - 1, 1).reshape(shape),
                pltpu.roll(here, width - 1, 1).reshape(shape),
            )
            down = jnp.where(
                lane == 0,
                pltpu.roll(west, 1, 1).reshape(shape),
                pltpu.roll(here, 1, 1).reshape(shape),
            )
            zonal.append(up - down)
            edges = jnp.dot(place, halo_recv[n, x], preferred_element_type=F32).reshape(shape) * outer
            weighted = here.reshape(shape) * cosine
            north = jnp.where(line == lat - 1, edges, pltpu.roll(weighted, lat - 1, 1))
            south = jnp.where(line == 0, edges, pltpu.roll(weighted, 1, 1))
            meridional.append(north - south)
        out_buf[n, 0] = ((zonal[1] - meridional[0]) * scale).reshape(rows, width)
        out_buf[n, 1] = ((zonal[0] + meridional[1]) * scale).reshape(rows, width)
        for copy in out_copies(n):
            copy.start()

    def finish(step, carry):
        @pl.when(step < chunks)
        def _():
            make_velocity(step)

        @pl.when(step >= 2)
        def _():
            stencil(lax.rem(step - 1, chunks))

        return carry

    lax.fori_loop(0, chunks + 2, finish, 0)

    def drain(n, carry):
        eof_remote(n).wait_send()
        part_copy(n).wait_send()

        @pl.when(has_low)
        def _():
            halo_down(n).wait_send()

        @pl.when(has_high)
        def _():
            halo_up(n).wait_send()

        for copy in out_copies(n):
            copy.wait()
        return carry

    lax.fori_loop(0, chunks, drain, 0)


def shards(pcs, st_eof, spatial_eof, land_sea):
    n_tm = lax.axis_size("tm")
    n_tile = lax.axis_size("tile")
    pairs, days = pcs.shape
    lags = st_eof.shape[1]
    lat, lon = land_sea.shape
    chan = spatial_eof.shape[1]
    rows = days * lat
    depth = chan * lat
    width = 256
    chunks = lon // width
    lag_pad = -(-lags // 128) * 128
    total_days = days * n_tm

    start = total_days - days - lax.axis_index("tm") * days
    placed = lax.dynamic_update_slice(
        jnp.zeros((8, total_days), F32), pcs[:, ::-1], (jnp.int32(0), start)
    )
    total_lat = lat * n_tile
    base = (lax.axis_index("tile") * lat).astype(F32)

    def cos_at(rows_at):
        return jnp.cos((-70.0 + 140.0 * (rows_at + 0.5) / total_lat) * (math.pi / 180.0))

    inner = cos_at(base + jnp.arange(lat, dtype=F32))
    place = jnp.arange(lat, dtype=F32)
    outer = jnp.where(
        place == 0, cos_at(base - 1.0), jnp.where(place == lat - 1, cos_at(base + lat), 0.0)
    )
    coef = jnp.broadcast_to(
        jnp.concatenate([inner, outer, 1.0 / (2.0 * inner)])[:, None], (3 * lat, width)
    )
    dims = (n_tm, n_tile, days, lat, width, chunks, lags, chan)
    dma = pltpu.SemaphoreType.DMA
    vmem = pl.BlockSpec(memory_space=pltpu.VMEM)
    hbm = pl.BlockSpec(memory_space=pl.ANY)
    vorticity, divergence = pl.pallas_call(
        functools.partial(kernel, dims),
        out_shape=[jax.ShapeDtypeStruct((rows, lon), F32)] * 2,
        in_specs=[vmem, hbm, hbm, vmem, vmem],
        out_specs=[hbm, hbm],
        scratch_shapes=[
            pltpu.VMEM((n_tm - 1, 8, total_days), F32),
            pltpu.VMEM((pairs, lag_pad, st_eof.shape[2]), F32),
            pltpu.VMEM((chunks, 2, 2 * depth, width), BF16),
            pltpu.VMEM((2, rows, 2 * depth), BF16),
            pltpu.VMEM((chunks, 2, rows, width), BF16),
            pltpu.VMEM((chunks, 2, rows, width), BF16),
            pltpu.VMEM((chunks, 2, rows, width), BF16),
            pltpu.VMEM((chunks, 2, 2 * days, width), BF16),
            pltpu.VMEM((chunks, 2, 2 * days, width), BF16),
            pltpu.VMEM((chunks, 2, rows, width), F32),
            dma,
            dma((n_tm - 1,)),
            dma((n_tm - 1,)),
            dma((chunks,)),
            dma((chunks,)),
            dma((chunks,)),
            dma((chunks,)),
            dma((chunks,)),
            dma((2, chunks)),
            dma((2, chunks)),
            dma((2, chunks)),
        ],
        compiler_params=pltpu.CompilerParams(
            collective_id=0, has_side_effects=True, vmem_limit_bytes=62 * 1024 * 1024
        ),
        name="reconstruct",
    )(placed, st_eof, spatial_eof.reshape(2, depth, lon), land_sea, coef)
    return vorticity.reshape(days, lat, lon), divergence.reshape(days, lat, lon)


def solution(mesh):
    return jax.shard_map(
        shards,
        mesh=mesh,
        in_specs=(P(None, "tm"), P(), P(None, "tm", "tile", None), P("tile", None)),
        out_specs=(P("tm", "tile", None), P("tm", "tile", None)),
        check_vma=False,
    )
```

```python
import functools
import math

import jax
import jax.numpy as jnp
from jax import lax
from jax.experimental import pallas as pl
from jax.experimental.pallas import tpu as pltpu
from jax.sharding import PartitionSpec as P

MESH = pl.DeviceIdType.MESH
F32 = jnp.float32
BF16 = jnp.bfloat16


def iota(shape, axis):
    return lax.broadcasted_iota(jnp.int32, shape, axis)


def kernel(
    dims,
    pcs_ref,
    st_ref,
    eof_ref,
    mask_ref,
    vort_ref,
    div_ref,
    pcs_slots,
    st_buf,
    eof_buf,
    mix,
    send_buf,
    recv_buf,
    vel,
    halo_send,
    halo_recv,
    out_buf,
    coef_ref,
    st_sem,
    pcs_ssem,
    pcs_rsem,
    eof_lsem,
    eof_ssem,
    eof_rsem,
    part_ssem,
    part_rsem,
    halo_ssem,
    halo_rsem,
    out_sem,
):
    n_tm, n_tile, days, lat, width, chunks, lags, chan = dims
    rows = days * lat
    depth = chan * lat
    me = lax.axis_index("tm")
    tile = lax.axis_index("tile")
    partner = me + 1 - 2 * lax.rem(me, 2)
    cross = lax.rem(me + n_tm // 2, n_tm)
    has_low = tile > 0
    has_high = tile < n_tile - 1

    st_copy = pltpu.make_async_copy(st_ref, st_buf.at[:, pl.ds(0, lags)], st_sem)
    st_copy.start()

    def eof_local(n):
        src = eof_ref.at[:, :, pl.ds(pl.multiple_of(n * width, width), width)]
        return pltpu.make_async_copy(src, eof_buf.at[n, :, pl.ds(0, depth)], eof_lsem.at[n])

    def eof_remote(n):
        src = eof_ref.at[:, :, pl.ds(pl.multiple_of(n * width, width), width)]
        return pltpu.make_async_remote_copy(
            src_ref=src,
            dst_ref=eof_buf.at[n, :, pl.ds(depth, depth)],
            send_sem=eof_ssem.at[n],
            recv_sem=eof_rsem.at[n],
            device_id=(partner, tile),
            device_id_type=MESH,
        )

    def part_copy(n, x):
        return pltpu.make_async_remote_copy(
            src_ref=send_buf.at[n, x],
            dst_ref=recv_buf.at[n, x],
            send_sem=part_ssem.at[x, n],
            recv_sem=part_rsem.at[x, n],
            device_id=(cross, tile),
            device_id_type=MESH,
        )

    def halo_down(n):
        return pltpu.make_async_remote_copy(
            src_ref=halo_send.at[n, :, pl.ds(0, days)],
            dst_ref=halo_recv.at[n, :, pl.ds(days, days)],
            send_sem=halo_ssem.at[0, n],
            recv_sem=halo_rsem.at[0, n],
            device_id=(me, tile - 1),
            device_id_type=MESH,
        )

    def halo_up(n):
        return pltpu.make_async_remote_copy(
            src_ref=halo_send.at[n, :, pl.ds(days, days)],
            dst_ref=halo_recv.at[n, :, pl.ds(0, days)],
            send_sem=halo_ssem.at[1, n],
            recv_sem=halo_rsem.at[1, n],
            device_id=(me, tile + 1),
            device_id_type=MESH,
        )

    def out_copies(n):
        cols = pl.ds(pl.multiple_of(n * width, width), width)
        return [
            pltpu.make_async_copy(out_buf.at[n, q], ref.at[:, cols], out_sem.at[q, n])
            for q, ref in enumerate((vort_ref, div_ref))
        ]

    lax.fori_loop(0, chunks, lambda n, c: (eof_local(n).start(), c)[1], 0)

    barrier = pltpu.get_barrier_semaphore()
    for step in range(1, n_tm):
        pl.semaphore_signal(
            barrier, inc=1, device_id=(lax.rem(me + step, n_tm), tile), device_id_type=MESH
        )

    @pl.when(has_low)
    def _():
        pl.semaphore_signal(barrier, inc=1, device_id=(me, tile - 1), device_id_type=MESH)

    @pl.when(has_high)
    def _():
        pl.semaphore_signal(barrier, inc=1, device_id=(me, tile + 1), device_id_type=MESH)

    neighbours = has_low.astype(jnp.int32) + has_high.astype(jnp.int32)
    pl.semaphore_wait(barrier, n_tm - 1 + neighbours)

    pcs_copies = []
    for step in range(1, n_tm):
        copy = pltpu.make_async_remote_copy(
            src_ref=pcs_ref,
            dst_ref=pcs_slots.at[step - 1],
            send_sem=pcs_ssem.at[step - 1],
            recv_sem=pcs_rsem.at[step - 1],
            device_id=(lax.rem(me + step, n_tm), tile),
            device_id_type=MESH,
        )
        copy.start()
        pcs_copies.append(copy)
    lax.fori_loop(0, chunks, lambda n, c: (eof_remote(n).start(), c)[1], 0)

    lag_pad = st_buf.shape[1]
    if lag_pad > lags:
        st_buf[:, lags:] = jnp.zeros((st_buf.shape[0], lag_pad - lags, st_buf.shape[2]), F32)

    @pl.when(jnp.logical_not(has_low))
    def _():
        halo_recv[:, :, pl.ds(0, days)] = jnp.zeros((chunks, 2, days, width), BF16)

    @pl.when(jnp.logical_not(has_high))
    def _():
        halo_recv[:, :, pl.ds(days, days)] = jnp.zeros((chunks, 2, days, width), BF16)

    st_copy.wait()
    for copy in pcs_copies:
        copy.wait()
    total_days = days * n_tm
    backward = jnp.zeros((st_buf.shape[0], total_days), F32)
    for step in range(n_tm):
        owner = lax.rem(me + n_tm - step, n_tm)
        days_of = pcs_ref[...] if step == 0 else pcs_slots[step - 1]
        at_day = iota((days, total_days), 0) + iota((days, total_days), 1)
        spot = (at_day == total_days - 1 - owner * days).astype(F32)
        backward = backward + jnp.dot(
            days_of, spot, precision=lax.Precision.HIGHEST, preferred_element_type=F32
        )

    repeat_rows = (
        (iota((rows, days), 0) >= iota((rows, days), 1) * lat)
        & (iota((rows, days), 0) < iota((rows, days), 1) * lat + lat)
    ).astype(BF16)
    piece = 2 * 128

    def build_mix(slot, target):
        first = target * days
        day = first + iota((days, lag_pad), 0)
        lag = iota((days, lag_pad), 1)
        inside = (lag <= day) & (lag < lags)
        lagged = []
        for k in range(st_buf.shape[0]):
            wide = jnp.broadcast_to(backward[k : k + 1], (days, total_days))
            wide = pltpu.roll(wide, first + 1, 1)
            at = iota((days, total_days), 0)
            bit = 1
            while bit < days:
                wide = jnp.where((at & bit) != 0, pltpu.roll(wide, bit, 1), wide)
                bit *= 2
            lagged.append(jnp.where(inside, wide[:, :lag_pad], 0.0))
        window = jnp.minimum(first + iota((days, chan), 0) + 1, lags).astype(F32)
        for part, owner in enumerate((me, partner)):
            cols = pl.ds(pl.multiple_of(owner * chan, chan), chan)
            sums = jnp.zeros((days, chan), F32)
            for k in range(st_buf.shape[0]):
                sums = sums + jnp.dot(
                    lagged[k],
                    st_buf[k, :, cols],
                    precision=lax.Precision.HIGHEST,
                    preferred_element_type=F32,
                )
            comp = (sums / window).astype(BF16)
            tall = jnp.dot(repeat_rows, comp, preferred_element_type=F32).astype(BF16)
            for start in range(0, depth, piece):
                c_at = iota((chan, piece), 0) * lat
                col_at = iota((chan, piece), 1) + start
                expand = ((col_at >= c_at) & (col_at < c_at + lat)).astype(BF16)
                spread = jnp.dot(tall, expand, preferred_element_type=F32)
                same = (iota((rows, piece), 0) & (lat - 1)) == (iota((rows, piece), 1) & (lat - 1))
                mix[slot, :, part * depth + start : part * depth + start + piece] = jnp.where(
                    same, spread, 0.0
                ).astype(BF16)

    build_mix(0, cross)

    def send_part(n, carry):
        eof_local(n).wait()
        eof_remote(n).wait_recv()
        for x in range(2):
            send_buf[n, x] = jnp.dot(
                mix[0], eof_buf[n, x], preferred_element_type=F32
            ).astype(BF16)
            part_copy(n, x).start()
        return carry

    lax.fori_loop(0, chunks, send_part, 0)
    build_mix(1, me)

    line_at = tile * lat + iota((lat, width), 0)
    at_line = iota((lat, width), 0)

    def cos_at(lines):
        degrees = -70.0 + 140.0 * (lines.astype(F32) + 0.5) / (lat * n_tile)
        return jnp.cos(degrees * (math.pi / 180.0))

    inner = cos_at(line_at)
    coef_ref[0:lat] = inner
    coef_ref[lat : 2 * lat] = jnp.where(
        at_line == 0,
        cos_at(line_at - 1),
        jnp.where(at_line == lat - 1, cos_at(line_at + 1), 0.0),
    )
    coef_ref[2 * lat : 3 * lat] = 1.0 / (2.0 * inner)

    edge = iota((2 * days, rows), 0)
    row = iota((2 * days, rows), 1)
    pick = ((edge < days) & (row == edge * lat)) | (
        (edge >= days) & (row == (edge - days) * lat + lat - 1)
    )
    edge_t = iota((rows, 2 * days), 1)
    row_t = iota((rows, 2 * days), 0)
    place = ((edge_t < days) & (row_t == edge_t * lat)) | (
        (edge_t >= days) & (row_t == (edge_t - days) * lat + lat - 1)
    )
    pick = pick.astype(BF16)
    place = place.astype(BF16)

    def make_velocity(n):
        own = [jnp.dot(mix[1], eof_buf[n, x], preferred_element_type=F32) for x in range(2)]
        ocean = mask_ref[:, pl.ds(pl.multiple_of(n * width, width), width)].astype(F32)
        for x in range(2):
            part_copy(n, x).wait_recv()
            total = (own[x] + recv_buf[n, x].astype(F32)).reshape(days, lat, width)
            vel[n, x] = (total * ocean[None]).reshape(rows, width).astype(BF16)
            halo_send[n, x] = jnp.dot(pick, vel[n, x], preferred_element_type=F32).astype(BF16)

        @pl.when(has_low)
        def _():
            halo_down(n).start()

        @pl.when(has_high)
        def _():
            halo_up(n).start()

    def stencil(n):
        before = lax.rem(n + chunks - 1, chunks)
        after = lax.rem(n + 1, chunks)

        @pl.when(has_low)
        def _():
            halo_up(n).wait_recv()

        @pl.when(has_high)
        def _():
            halo_down(n).wait_recv()

        shape = (days, lat, width)
        lane = iota((lat, width), 1)[None]
        line = iota((lat, width), 0)[None]
        cosine = coef_ref[0:lat][None]
        outer = coef_ref[lat : 2 * lat][None]
        ocean = mask_ref[:, pl.ds(pl.multiple_of(n * width, width), width)].astype(F32)
        scale = (ocean * coef_ref[2 * lat : 3 * lat])[None]
        zonal = []
        meridional = []
        for x in range(2):
            here = vel[n, x].astype(F32).reshape(rows, width)
            west = vel[before, x].astype(F32)
            east = vel[after, x].astype(F32)
            up = jnp.where(
                lane == width - 1,
                pltpu.roll(east, width - 1, 1).reshape(shape),
                pltpu.roll(here, width - 1, 1).reshape(shape),
            )
            down = jnp.where(
                lane == 0,
                pltpu.roll(west, 1, 1).reshape(shape),
                pltpu.roll(here, 1, 1).reshape(shape),
            )
            zonal.append(up - down)
            edges = jnp.dot(place, halo_recv[n, x], preferred_element_type=F32).reshape(shape) * outer
            weighted = here.reshape(shape) * cosine
            north = jnp.where(line == lat - 1, edges, pltpu.roll(weighted, lat - 1, 1))
            south = jnp.where(line == 0, edges, pltpu.roll(weighted, 1, 1))
            meridional.append(north - south)
        out_buf[n, 0] = ((zonal[1] - meridional[0]) * scale).reshape(rows, width)
        out_buf[n, 1] = ((zonal[0] + meridional[1]) * scale).reshape(rows, width)
        for copy in out_copies(n):
            copy.start()

    def finish(step, carry):
        @pl.when(step < chunks)
        def _():
            make_velocity(step)

        @pl.when(step >= 2)
        def _():
            stencil(jnp.where(step >= chunks, (step - chunks) * (chunks - 1), step - 1))

        return carry

    lax.fori_loop(0, chunks + 2, finish, 0)

    def drain(n, carry):
        eof_remote(n).wait_send()
        for x in range(2):
            part_copy(n, x).wait_send()

        @pl.when(has_low)
        def _():
            halo_down(n).wait_send()

        @pl.when(has_high)
        def _():
            halo_up(n).wait_send()

        for copy in out_copies(n):
            copy.wait()
        return carry

    lax.fori_loop(0, chunks, drain, 0)


def shards(pcs, st_eof, spatial_eof, land_sea):
    n_tm = lax.axis_size("tm")
    n_tile = lax.axis_size("tile")
    pairs, days = pcs.shape
    lags = st_eof.shape[1]
    lat, lon = land_sea.shape
    chan = spatial_eof.shape[1]
    rows = days * lat
    depth = chan * lat
    width = 256
    chunks = lon // width
    lag_pad = -(-lags // 128) * 128
    dims = (n_tm, n_tile, days, lat, width, chunks, lags, chan)
    dma = pltpu.SemaphoreType.DMA
    vmem = pl.BlockSpec(memory_space=pltpu.VMEM)
    hbm = pl.BlockSpec(memory_space=pl.ANY)
    vorticity, divergence = pl.pallas_call(
        functools.partial(kernel, dims),
        out_shape=[jax.ShapeDtypeStruct((rows, lon), F32)] * 2,
        in_specs=[vmem, hbm, hbm, vmem],
        out_specs=[hbm, hbm],
        scratch_shapes=[
            pltpu.VMEM((n_tm - 1, pairs, days), F32),
            pltpu.VMEM((pairs, lag_pad, st_eof.shape[2]), F32),
            pltpu.VMEM((chunks, 2, 2 * depth, width), BF16),
            pltpu.VMEM((2, rows, 2 * depth), BF16),
            pltpu.VMEM((chunks, 2, rows, width), BF16),
            pltpu.VMEM((chunks, 2, rows, width), BF16),
            pltpu.VMEM((chunks, 2, rows, width), BF16),
            pltpu.VMEM((chunks, 2, 2 * days, width), BF16),
            pltpu.VMEM((chunks, 2, 2 * days, width), BF16),
            pltpu.VMEM((chunks, 2, rows, width), F32),
            pltpu.VMEM((3 * lat, width), F32),
            dma,
            dma((n_tm - 1,)),
            dma((n_tm - 1,)),
            dma((chunks,)),
            dma((chunks,)),
            dma((chunks,)),
            dma((2, chunks)),
            dma((2, chunks)),
            dma((2, chunks)),
            dma((2, chunks)),
            dma((2, chunks)),
        ],
        compiler_params=pltpu.CompilerParams(
            collective_id=0, has_side_effects=True, vmem_limit_bytes=62 * 1024 * 1024
        ),
        name="reconstruct",
    )(pcs, st_eof, spatial_eof.reshape(2, depth, lon), land_sea)
    return vorticity.reshape(days, lat, lon), divergence.reshape(days, lat, lon)


def solution(mesh):
    return jax.shard_map(
        shards,
        mesh=mesh,
        in_specs=(P(None, "tm"), P(), P(None, "tm", "tile", None), P("tile", None)),
        out_specs=(P("tm", "tile", None), P("tm", "tile", None)),
        check_vma=False,
    )
```

```python
import functools
import math

import jax
import jax.numpy as jnp
from jax import lax
from jax.experimental import pallas as pl
from jax.experimental.pallas import tpu as pltpu
from jax.sharding import PartitionSpec as P

MESH = pl.DeviceIdType.MESH
F32 = jnp.float32
BF16 = jnp.bfloat16


def iota(shape, axis):
    return lax.broadcasted_iota(jnp.int32, shape, axis)


def kernel(
    dims,
    pcs_ref,
    st_ref,
    eof_ref,
    mask_ref,
    vort_ref,
    div_ref,
    pcs_slots,
    st_buf,
    eof_buf,
    mix,
    send_buf,
    recv_buf,
    vel,
    halo_send,
    halo_recv,
    out_buf,
    coef_ref,
    edge_buf,
    st_sem,
    pcs_ssem,
    pcs_rsem,
    eof_lsem,
    eof_ssem,
    eof_rsem,
    part_ssem,
    part_rsem,
    halo_ssem,
    halo_rsem,
    out_sem,
):
    n_tm, n_tile, days, lat, width, chunks, lags, chan = dims
    rows = days * lat
    depth = chan * lat
    me = lax.axis_index("tm")
    tile = lax.axis_index("tile")
    partner = me + 1 - 2 * lax.rem(me, 2)
    cross = lax.rem(me + n_tm // 2, n_tm)
    has_low = tile > 0
    has_high = tile < n_tile - 1

    st_copy = pltpu.make_async_copy(st_ref, st_buf.at[:, pl.ds(0, lags)], st_sem)
    st_copy.start()

    def eof_local(n):
        src = eof_ref.at[:, :, pl.ds(pl.multiple_of(n * width, width), width)]
        return pltpu.make_async_copy(src, eof_buf.at[n, :, pl.ds(0, depth)], eof_lsem.at[n])

    def eof_remote(n):
        src = eof_ref.at[:, :, pl.ds(pl.multiple_of(n * width, width), width)]
        return pltpu.make_async_remote_copy(
            src_ref=src,
            dst_ref=eof_buf.at[n, :, pl.ds(depth, depth)],
            send_sem=eof_ssem.at[n],
            recv_sem=eof_rsem.at[n],
            device_id=(partner, tile),
            device_id_type=MESH,
        )

    def part_copy(n, x):
        return pltpu.make_async_remote_copy(
            src_ref=send_buf.at[n, x],
            dst_ref=recv_buf.at[n, x],
            send_sem=part_ssem.at[x, n],
            recv_sem=part_rsem.at[x, n],
            device_id=(cross, tile),
            device_id_type=MESH,
        )

    def halo_down(n):
        return pltpu.make_async_remote_copy(
            src_ref=halo_send.at[n, :, pl.ds(0, days)],
            dst_ref=halo_recv.at[n, :, pl.ds(days, days)],
            send_sem=halo_ssem.at[0, n],
            recv_sem=halo_rsem.at[0, n],
            device_id=(me, tile - 1),
            device_id_type=MESH,
        )

    def halo_up(n):
        return pltpu.make_async_remote_copy(
            src_ref=halo_send.at[n, :, pl.ds(days, days)],
            dst_ref=halo_recv.at[n, :, pl.ds(0, days)],
            send_sem=halo_ssem.at[1, n],
            recv_sem=halo_rsem.at[1, n],
            device_id=(me, tile + 1),
            device_id_type=MESH,
        )

    def out_copies(n):
        cols = pl.ds(pl.multiple_of(n * width, width), width)
        return [
            pltpu.make_async_copy(out_buf.at[n, q], ref.at[:, cols], out_sem.at[q, n])
            for q, ref in enumerate((vort_ref, div_ref))
        ]

    lax.fori_loop(0, chunks, lambda n, c: (eof_local(n).start(), c)[1], 0)

    barrier = pltpu.get_barrier_semaphore()
    for step in range(1, n_tm):
        pl.semaphore_signal(
            barrier, inc=1, device_id=(lax.rem(me + step, n_tm), tile), device_id_type=MESH
        )

    @pl.when(has_low)
    def _():
        pl.semaphore_signal(barrier, inc=1, device_id=(me, tile - 1), device_id_type=MESH)

    @pl.when(has_high)
    def _():
        pl.semaphore_signal(barrier, inc=1, device_id=(me, tile + 1), device_id_type=MESH)

    neighbours = has_low.astype(jnp.int32) + has_high.astype(jnp.int32)
    pl.semaphore_wait(barrier, n_tm - 1 + neighbours)

    pcs_copies = []
    for step in range(1, n_tm):
        copy = pltpu.make_async_remote_copy(
            src_ref=pcs_ref,
            dst_ref=pcs_slots.at[step - 1],
            send_sem=pcs_ssem.at[step - 1],
            recv_sem=pcs_rsem.at[step - 1],
            device_id=(lax.rem(me + step, n_tm), tile),
            device_id_type=MESH,
        )
        copy.start()
        pcs_copies.append(copy)
    lax.fori_loop(0, chunks, lambda n, c: (eof_remote(n).start(), c)[1], 0)

    lag_pad = st_buf.shape[1]
    if lag_pad > lags:
        st_buf[:, lags:] = jnp.zeros((st_buf.shape[0], lag_pad - lags, st_buf.shape[2]), F32)

    @pl.when(jnp.logical_not(has_low))
    def _():
        halo_recv[:, :, pl.ds(0, days)] = jnp.zeros((chunks, 2, days, width), BF16)

    @pl.when(jnp.logical_not(has_high))
    def _():
        halo_recv[:, :, pl.ds(days, days)] = jnp.zeros((chunks, 2, days, width), BF16)

    st_copy.wait()
    for copy in pcs_copies:
        copy.wait()
    total_days = days * n_tm
    backward = jnp.zeros((st_buf.shape[0], total_days), F32)
    for step in range(n_tm):
        owner = lax.rem(me + n_tm - step, n_tm)
        days_of = pcs_ref[...] if step == 0 else pcs_slots[step - 1]
        at_day = iota((days, total_days), 0) + iota((days, total_days), 1)
        spot = (at_day == total_days - 1 - owner * days).astype(F32)
        backward = backward + jnp.dot(
            days_of, spot, precision=lax.Precision.HIGHEST, preferred_element_type=F32
        )

    repeat_rows = (
        (iota((rows, days), 0) >= iota((rows, days), 1) * lat)
        & (iota((rows, days), 0) < iota((rows, days), 1) * lat + lat)
    ).astype(BF16)
    piece = 2 * 128

    def build_mix(slot, target):
        first = target * days
        day = first + iota((days, lag_pad), 0)
        lag = iota((days, lag_pad), 1)
        inside = (lag <= day) & (lag < lags)
        lagged = []
        for k in range(st_buf.shape[0]):
            wide = jnp.broadcast_to(backward[k : k + 1], (days, total_days))
            wide = pltpu.roll(wide, first + 1, 1)
            at = iota((days, total_days), 0)
            bit = 1
            while bit < days:
                wide = jnp.where((at & bit) != 0, pltpu.roll(wide, bit, 1), wide)
                bit *= 2
            lagged.append(jnp.where(inside, wide[:, :lag_pad], 0.0))
        window = jnp.minimum(first + iota((days, chan), 0) + 1, lags).astype(F32)
        for part, owner in enumerate((me, partner)):
            cols = pl.ds(pl.multiple_of(owner * chan, chan), chan)
            sums = jnp.zeros((days, chan), F32)
            for k in range(st_buf.shape[0]):
                sums = sums + jnp.dot(
                    lagged[k],
                    st_buf[k, :, cols],
                    precision=lax.Precision.HIGHEST,
                    preferred_element_type=F32,
                )
            comp = (sums / window).astype(BF16)
            tall = jnp.dot(repeat_rows, comp, preferred_element_type=F32).astype(BF16)
            for start in range(0, depth, piece):
                c_at = iota((chan, piece), 0) * lat
                col_at = iota((chan, piece), 1) + start
                expand = ((col_at >= c_at) & (col_at < c_at + lat)).astype(BF16)
                spread = jnp.dot(tall, expand, preferred_element_type=F32)
                same = (iota((rows, piece), 0) & (lat - 1)) == (iota((rows, piece), 1) & (lat - 1))
                mix[slot, :, part * depth + start : part * depth + start + piece] = jnp.where(
                    same, spread, 0.0
                ).astype(BF16)

    build_mix(0, cross)

    def send_part(n, carry):
        eof_local(n).wait()
        eof_remote(n).wait_recv()
        for x in range(2):
            send_buf[n, x] = jnp.dot(
                mix[0], eof_buf[n, x], preferred_element_type=F32
            ).astype(BF16)
            part_copy(n, x).start()
        return carry

    lax.fori_loop(0, chunks, send_part, 0)
    build_mix(1, me)

    line_at = tile * lat + iota((lat, width), 0)
    at_line = iota((lat, width), 0)

    def cos_at(lines):
        degrees = -70.0 + 140.0 * (lines.astype(F32) + 0.5) / (lat * n_tile)
        return jnp.cos(degrees * (math.pi / 180.0))

    inner = cos_at(line_at)
    coef_ref[0:lat] = inner
    coef_ref[lat : 2 * lat] = jnp.where(
        at_line == 0,
        cos_at(line_at - 1),
        jnp.where(at_line == lat - 1, cos_at(line_at + 1), 0.0),
    )
    coef_ref[2 * lat : 3 * lat] = 1.0 / (2.0 * inner)

    edge = iota((2 * days, rows), 0)
    row = iota((2 * days, rows), 1)
    pick = ((edge < days) & (row == edge * lat)) | (
        (edge >= days) & (row == (edge - days) * lat + lat - 1)
    )
    edge_t = iota((rows, 2 * days), 1)
    row_t = iota((rows, 2 * days), 0)
    place = ((edge_t < days) & (row_t == edge_t * lat)) | (
        (edge_t >= days) & (row_t == (edge_t - days) * lat + lat - 1)
    )
    pick = pick.astype(BF16)
    place = place.astype(BF16)

    def make_velocity(n):
        own = [jnp.dot(mix[1], eof_buf[n, x], preferred_element_type=F32) for x in range(2)]
        ocean = mask_ref[:, pl.ds(pl.multiple_of(n * width, width), width)].astype(F32)
        for x in range(2):
            part_copy(n, x).wait_recv()
            total = (own[x] + recv_buf[n, x].astype(F32)).reshape(days, lat, width)
            vel[n, x] = (total * ocean[None]).reshape(rows, width).astype(BF16)
            halo_send[n, x] = jnp.dot(pick, vel[n, x], preferred_element_type=F32).astype(BF16)

        @pl.when(has_low)
        def _():
            halo_down(n).start()

        @pl.when(has_high)
        def _():
            halo_up(n).start()

    def stencil(n):
        before = lax.rem(n + chunks - 1, chunks)
        after = lax.rem(n + 1, chunks)

        @pl.when(has_low)
        def _():
            halo_up(n).wait_recv()

        @pl.when(has_high)
        def _():
            halo_down(n).wait_recv()

        for x in range(2):
            edge_buf[x] = jnp.dot(place, halo_recv[n, x], preferred_element_type=F32)
        group = 4 * lat
        shape = (4, lat, width)
        lane = iota((lat, width), 1)[None]
        line = iota((lat, width), 0)[None]
        cosine = coef_ref[0:lat][None]
        outer = coef_ref[lat : 2 * lat][None]
        ocean = mask_ref[:, pl.ds(pl.multiple_of(n * width, width), width)].astype(F32)
        scale = (ocean * coef_ref[2 * lat : 3 * lat])[None]

        def days_of(b, carry):
            at = pl.ds(pl.multiple_of(b * group, group), group)
            zonal = []
            meridional = []
            for x in range(2):
                here = vel[n, x, at].astype(F32)
                west = vel[before, x, at, width - 128 :].astype(F32)
                east = vel[after, x, at, :128].astype(F32)
                west = jnp.concatenate([pltpu.roll(west, 1, 1), here[:, 128:]], axis=1)
                east = jnp.concatenate([here[:, :-128], pltpu.roll(east, 127, 1)], axis=1)
                up = jnp.where(
                    lane == width - 1,
                    east.reshape(shape),
                    pltpu.roll(here, width - 1, 1).reshape(shape),
                )
                down = jnp.where(
                    lane == 0, west.reshape(shape), pltpu.roll(here, 1, 1).reshape(shape)
                )
                zonal.append(up - down)
                edges = edge_buf[x, at].reshape(shape) * outer
                weighted = here.reshape(shape) * cosine
                north = jnp.where(line == lat - 1, edges, pltpu.roll(weighted, lat - 1, 1))
                south = jnp.where(line == 0, edges, pltpu.roll(weighted, 1, 1))
                meridional.append(north - south)
            out_buf[n, 0, at] = ((zonal[1] - meridional[0]) * scale).reshape(group, width)
            out_buf[n, 1, at] = ((zonal[0] + meridional[1]) * scale).reshape(group, width)
            return carry

        lax.fori_loop(0, rows // group, days_of, 0)
        for copy in out_copies(n):
            copy.start()

    def finish(step, carry):
        @pl.when(step < chunks)
        def _():
            make_velocity(step)

        @pl.when(step >= 2)
        def _():
            stencil(jnp.where(step >= chunks, (step - chunks) * (chunks - 1), step - 1))

        return carry

    lax.fori_loop(0, chunks + 2, finish, 0)

    def drain(n, carry):
        eof_remote(n).wait_send()
        for x in range(2):
            part_copy(n, x).wait_send()

        @pl.when(has_low)
        def _():
            halo_down(n).wait_send()

        @pl.when(has_high)
        def _():
            halo_up(n).wait_send()

        for copy in out_copies(n):
            copy.wait()
        return carry

    lax.fori_loop(0, chunks, drain, 0)


def shards(pcs, st_eof, spatial_eof, land_sea):
    n_tm = lax.axis_size("tm")
    n_tile = lax.axis_size("tile")
    pairs, days = pcs.shape
    lags = st_eof.shape[1]
    lat, lon = land_sea.shape
    chan = spatial_eof.shape[1]
    rows = days * lat
    depth = chan * lat
    width = 256
    chunks = lon // width
    lag_pad = -(-lags // 128) * 128
    dims = (n_tm, n_tile, days, lat, width, chunks, lags, chan)
    dma = pltpu.SemaphoreType.DMA
    vmem = pl.BlockSpec(memory_space=pltpu.VMEM)
    hbm = pl.BlockSpec(memory_space=pl.ANY)
    vorticity, divergence = pl.pallas_call(
        functools.partial(kernel, dims),
        out_shape=[jax.ShapeDtypeStruct((rows, lon), F32)] * 2,
        in_specs=[vmem, hbm, hbm, vmem],
        out_specs=[hbm, hbm],
        scratch_shapes=[
            pltpu.VMEM((n_tm - 1, pairs, days), F32),
            pltpu.VMEM((pairs, lag_pad, st_eof.shape[2]), F32),
            pltpu.VMEM((chunks, 2, 2 * depth, width), BF16),
            pltpu.VMEM((2, rows, 2 * depth), BF16),
            pltpu.VMEM((chunks, 2, rows, width), BF16),
            pltpu.VMEM((chunks, 2, rows, width), BF16),
            pltpu.VMEM((chunks, 2, rows, width), BF16),
            pltpu.VMEM((chunks, 2, 2 * days, width), BF16),
            pltpu.VMEM((chunks, 2, 2 * days, width), BF16),
            pltpu.VMEM((chunks, 2, rows, width), F32),
            pltpu.VMEM((3 * lat, width), F32),
            pltpu.VMEM((2, rows, width), F32),
            dma,
            dma((n_tm - 1,)),
            dma((n_tm - 1,)),
            dma((chunks,)),
            dma((chunks,)),
            dma((chunks,)),
            dma((2, chunks)),
            dma((2, chunks)),
            dma((2, chunks)),
            dma((2, chunks)),
            dma((2, chunks)),
        ],
        compiler_params=pltpu.CompilerParams(
            collective_id=0, has_side_effects=True, vmem_limit_bytes=62 * 1024 * 1024
        ),
        name="reconstruct",
    )(pcs, st_eof, spatial_eof.reshape(2, depth, lon), land_sea)
    return vorticity.reshape(days, lat, lon), divergence.reshape(days, lat, lon)


def solution(mesh):
    return jax.shard_map(
        shards,
        mesh=mesh,
        in_specs=(P(None, "tm"), P(), P(None, "tm", "tile", None), P("tile", None)),
        out_specs=(P("tm", "tile", None), P("tm", "tile", None)),
        check_vma=False,
    )
```

```python
import functools
import math

import jax
import jax.numpy as jnp
from jax import lax
from jax.experimental import pallas as pl
from jax.experimental.pallas import tpu as pltpu
from jax.sharding import PartitionSpec as P

MESH = pl.DeviceIdType.MESH
F32 = jnp.float32
BF16 = jnp.bfloat16


def iota(shape, axis):
    return lax.broadcasted_iota(jnp.int32, shape, axis)


def kernel(
    dims,
    pcs_ref,
    st_ref,
    eof_ref,
    mask_ref,
    vort_ref,
    div_ref,
    pcs_slots,
    st_buf,
    eof_buf,
    mix,
    send_buf,
    recv_buf,
    vel,
    halo_send,
    halo_recv,
    out_buf,
    coef_ref,
    st_sem,
    pcs_ssem,
    pcs_rsem,
    eof_lsem,
    eof_ssem,
    eof_rsem,
    part_ssem,
    part_rsem,
    halo_ssem,
    halo_rsem,
    out_sem,
):
    n_tm, n_tile, days, lat, width, chunks, lags, chan = dims
    rows = days * lat
    depth = chan * lat
    me = lax.axis_index("tm")
    tile = lax.axis_index("tile")
    partner = me + 1 - 2 * lax.rem(me, 2)
    cross = lax.rem(me + n_tm // 2, n_tm)
    has_low = tile > 0
    has_high = tile < n_tile - 1

    st_copy = pltpu.make_async_copy(st_ref, st_buf.at[:, pl.ds(0, lags)], st_sem)
    st_copy.start()

    def eof_local(n, x):
        src = eof_ref.at[x, :, pl.ds(pl.multiple_of(n * width, width), width)]
        return pltpu.make_async_copy(src, eof_buf.at[n, x, pl.ds(0, depth)], eof_lsem.at[x, n])

    def eof_remote(n, x):
        src = eof_ref.at[x, :, pl.ds(pl.multiple_of(n * width, width), width)]
        return pltpu.make_async_remote_copy(
            src_ref=src,
            dst_ref=eof_buf.at[n, x, pl.ds(depth, depth)],
            send_sem=eof_ssem.at[x, n],
            recv_sem=eof_rsem.at[x, n],
            device_id=(partner, tile),
            device_id_type=MESH,
        )

    def part_copy(n, x):
        return pltpu.make_async_remote_copy(
            src_ref=send_buf.at[n, x],
            dst_ref=recv_buf.at[n, x],
            send_sem=part_ssem.at[x, n],
            recv_sem=part_rsem.at[x, n],
            device_id=(cross, tile),
            device_id_type=MESH,
        )

    def halo_down(n):
        return pltpu.make_async_remote_copy(
            src_ref=halo_send.at[n, :, pl.ds(0, days)],
            dst_ref=halo_recv.at[n, :, pl.ds(days, days)],
            send_sem=halo_ssem.at[0, n],
            recv_sem=halo_rsem.at[0, n],
            device_id=(me, tile - 1),
            device_id_type=MESH,
        )

    def halo_up(n):
        return pltpu.make_async_remote_copy(
            src_ref=halo_send.at[n, :, pl.ds(days, days)],
            dst_ref=halo_recv.at[n, :, pl.ds(0, days)],
            send_sem=halo_ssem.at[1, n],
            recv_sem=halo_rsem.at[1, n],
            device_id=(me, tile + 1),
            device_id_type=MESH,
        )

    def out_copies(n):
        cols = pl.ds(pl.multiple_of(n * width, width), width)
        return [
            pltpu.make_async_copy(out_buf.at[n, q], ref.at[:, cols], out_sem.at[q, n])
            for q, ref in enumerate((vort_ref, div_ref))
        ]

    lax.fori_loop(
        0, chunks, lambda n, c: (eof_local(n, 0).start(), eof_local(n, 1).start(), c)[2], 0
    )

    barrier = pltpu.get_barrier_semaphore()
    for step in range(1, n_tm):
        pl.semaphore_signal(
            barrier, inc=1, device_id=(lax.rem(me + step, n_tm), tile), device_id_type=MESH
        )

    @pl.when(has_low)
    def _():
        pl.semaphore_signal(barrier, inc=1, device_id=(me, tile - 1), device_id_type=MESH)

    @pl.when(has_high)
    def _():
        pl.semaphore_signal(barrier, inc=1, device_id=(me, tile + 1), device_id_type=MESH)

    neighbours = has_low.astype(jnp.int32) + has_high.astype(jnp.int32)
    pl.semaphore_wait(barrier, n_tm - 1 + neighbours)

    pcs_copies = []
    for step in range(1, n_tm):
        copy = pltpu.make_async_remote_copy(
            src_ref=pcs_ref,
            dst_ref=pcs_slots.at[step - 1],
            send_sem=pcs_ssem.at[step - 1],
            recv_sem=pcs_rsem.at[step - 1],
            device_id=(lax.rem(me + step, n_tm), tile),
            device_id_type=MESH,
        )
        copy.start()
        pcs_copies.append(copy)
    lax.fori_loop(
        0, chunks, lambda n, c: (eof_remote(n, 0).start(), eof_remote(n, 1).start(), c)[2], 0
    )

    lag_pad = st_buf.shape[1]
    if lag_pad > lags:
        st_buf[:, lags:] = jnp.zeros((st_buf.shape[0], lag_pad - lags, st_buf.shape[2]), F32)

    @pl.when(jnp.logical_not(has_low))
    def _():
        halo_recv[:, :, pl.ds(0, days)] = jnp.zeros((chunks, 2, days, width), BF16)

    @pl.when(jnp.logical_not(has_high))
    def _():
        halo_recv[:, :, pl.ds(days, days)] = jnp.zeros((chunks, 2, days, width), BF16)

    st_copy.wait()
    for copy in pcs_copies:
        copy.wait()
    total_days = days * n_tm
    backward = jnp.zeros((st_buf.shape[0], total_days), F32)
    for step in range(n_tm):
        owner = lax.rem(me + n_tm - step, n_tm)
        days_of = pcs_ref[...] if step == 0 else pcs_slots[step - 1]
        at_day = iota((days, total_days), 0) + iota((days, total_days), 1)
        spot = (at_day == total_days - 1 - owner * days).astype(F32)
        backward = backward + jnp.dot(
            days_of, spot, precision=lax.Precision.HIGHEST, preferred_element_type=F32
        )

    repeat_rows = (
        (iota((rows, days), 0) >= iota((rows, days), 1) * lat)
        & (iota((rows, days), 0) < iota((rows, days), 1) * lat + lat)
    ).astype(BF16)
    piece = 2 * 128

    def build_mix(slot, target):
        first = target * days
        day = first + iota((days, lag_pad), 0)
        lag = iota((days, lag_pad), 1)
        inside = (lag <= day) & (lag < lags)
        lagged = []
        for k in range(st_buf.shape[0]):
            wide = jnp.broadcast_to(backward[k : k + 1], (days, total_days))
            wide = pltpu.roll(wide, first + 1, 1)
            at = iota((days, total_days), 0)
            bit = 1
            while bit < days:
                wide = jnp.where((at & bit) != 0, pltpu.roll(wide, bit, 1), wide)
                bit *= 2
            lagged.append(jnp.where(inside, wide[:, :lag_pad], 0.0))
        window = jnp.minimum(first + iota((days, chan), 0) + 1, lags).astype(F32)
        for part, owner in enumerate((me, partner)):
            cols = pl.ds(pl.multiple_of(owner * chan, chan), chan)
            sums = jnp.zeros((days, chan), F32)
            for k in range(st_buf.shape[0]):
                sums = sums + jnp.dot(
                    lagged[k],
                    st_buf[k, :, cols],
                    precision=lax.Precision.HIGHEST,
                    preferred_element_type=F32,
                )
            comp = (sums / window).astype(BF16)
            tall = jnp.dot(repeat_rows, comp, preferred_element_type=F32).astype(BF16)
            for start in range(0, depth, piece):
                c_at = iota((chan, piece), 0) * lat
                col_at = iota((chan, piece), 1) + start
                expand = ((col_at >= c_at) & (col_at < c_at + lat)).astype(BF16)
                spread = jnp.dot(tall, expand, preferred_element_type=F32)
                same = (iota((rows, piece), 0) & (lat - 1)) == (iota((rows, piece), 1) & (lat - 1))
                mix[slot, :, part * depth + start : part * depth + start + piece] = jnp.where(
                    same, spread, 0.0
                ).astype(BF16)

    build_mix(0, cross)

    def send_part(n, carry):
        for x in range(2):
            eof_local(n, x).wait()
            eof_remote(n, x).wait_recv()
            send_buf[n, x] = jnp.dot(
                mix[0], eof_buf[n, x], preferred_element_type=F32
            ).astype(BF16)
            part_copy(n, x).start()
        return carry

    lax.fori_loop(0, chunks, send_part, 0)
    build_mix(1, me)

    line_at = tile * lat + iota((lat, width), 0)
    at_line = iota((lat, width), 0)

    def cos_at(lines):
        degrees = -70.0 + 140.0 * (lines.astype(F32) + 0.5) / (lat * n_tile)
        return jnp.cos(degrees * (math.pi / 180.0))

    inner = cos_at(line_at)
    coef_ref[0:lat] = inner
    coef_ref[lat : 2 * lat] = jnp.where(
        at_line == 0,
        cos_at(line_at - 1),
        jnp.where(at_line == lat - 1, cos_at(line_at + 1), 0.0),
    )
    coef_ref[2 * lat : 3 * lat] = 1.0 / (2.0 * inner)

    edge = iota((2 * days, rows), 0)
    row = iota((2 * days, rows), 1)
    pick = ((edge < days) & (row == edge * lat)) | (
        (edge >= days) & (row == (edge - days) * lat + lat - 1)
    )
    edge_t = iota((rows, 2 * days), 1)
    row_t = iota((rows, 2 * days), 0)
    place = ((edge_t < days) & (row_t == edge_t * lat)) | (
        (edge_t >= days) & (row_t == (edge_t - days) * lat + lat - 1)
    )
    pick = pick.astype(BF16)
    place = place.astype(BF16)

    def make_velocity(n):
        own = [jnp.dot(mix[1], eof_buf[n, x], preferred_element_type=F32) for x in range(2)]
        ocean = mask_ref[:, pl.ds(pl.multiple_of(n * width, width), width)].astype(F32)
        for x in range(2):
            part_copy(n, x).wait_recv()
            total = (own[x] + recv_buf[n, x].astype(F32)).reshape(days, lat, width)
            vel[n, x] = (total * ocean[None]).reshape(rows, width).astype(BF16)
            halo_send[n, x] = jnp.dot(pick, vel[n, x], preferred_element_type=F32).astype(BF16)

        @pl.when(has_low)
        def _():
            halo_down(n).start()

        @pl.when(has_high)
        def _():
            halo_up(n).start()

    def stencil(n):
        before = lax.rem(n + chunks - 1, chunks)
        after = lax.rem(n + 1, chunks)

        @pl.when(has_low)
        def _():
            halo_up(n).wait_recv()

        @pl.when(has_high)
        def _():
            halo_down(n).wait_recv()

        shape = (days, lat, width)
        lane = iota((lat, width), 1)[None]
        line = iota((lat, width), 0)[None]
        cosine = coef_ref[0:lat][None]
        outer = coef_ref[lat : 2 * lat][None]
        ocean = mask_ref[:, pl.ds(pl.multiple_of(n * width, width), width)].astype(F32)
        scale = (ocean * coef_ref[2 * lat : 3 * lat])[None]
        zonal = []
        meridional = []
        for x in range(2):
            here = vel[n, x].astype(F32).reshape(rows, width)
            west = vel[before, x].astype(F32)
            east = vel[after, x].astype(F32)
            up = jnp.where(
                lane == width - 1,
                pltpu.roll(east, width - 1, 1).reshape(shape),
                pltpu.roll(here, width - 1, 1).reshape(shape),
            )
            down = jnp.where(
                lane == 0,
                pltpu.roll(west, 1, 1).reshape(shape),
                pltpu.roll(here, 1, 1).reshape(shape),
            )
            zonal.append(up - down)
            edges = jnp.dot(place, halo_recv[n, x], preferred_element_type=F32).reshape(shape) * outer
            weighted = here.reshape(shape) * cosine
            north = jnp.where(line == lat - 1, edges, pltpu.roll(weighted, lat - 1, 1))
            south = jnp.where(line == 0, edges, pltpu.roll(weighted, 1, 1))
            meridional.append(north - south)
        out_buf[n, 0] = ((zonal[1] - meridional[0]) * scale).reshape(rows, width)
        out_buf[n, 1] = ((zonal[0] + meridional[1]) * scale).reshape(rows, width)
        for copy in out_copies(n):
            copy.start()

    def finish(step, carry):
        @pl.when(step < chunks)
        def _():
            make_velocity(step)

        @pl.when(step >= 2)
        def _():
            stencil(jnp.where(step >= chunks, (step - chunks) * (chunks - 1), step - 1))

        return carry

    lax.fori_loop(0, chunks + 2, finish, 0)

    def drain(n, carry):
        for x in range(2):
            eof_remote(n, x).wait_send()
            part_copy(n, x).wait_send()

        @pl.when(has_low)
        def _():
            halo_down(n).wait_send()

        @pl.when(has_high)
        def _():
            halo_up(n).wait_send()

        for copy in out_copies(n):
            copy.wait()
        return carry

    lax.fori_loop(0, chunks, drain, 0)


def shards(pcs, st_eof, spatial_eof, land_sea):
    n_tm = lax.axis_size("tm")
    n_tile = lax.axis_size("tile")
    pairs, days = pcs.shape
    lags = st_eof.shape[1]
    lat, lon = land_sea.shape
    chan = spatial_eof.shape[1]
    rows = days * lat
    depth = chan * lat
    width = 256
    chunks = lon // width
    lag_pad = -(-lags // 128) * 128
    dims = (n_tm, n_tile, days, lat, width, chunks, lags, chan)
    dma = pltpu.SemaphoreType.DMA
    vmem = pl.BlockSpec(memory_space=pltpu.VMEM)
    hbm = pl.BlockSpec(memory_space=pl.ANY)
    vorticity, divergence = pl.pallas_call(
        functools.partial(kernel, dims),
        out_shape=[jax.ShapeDtypeStruct((rows, lon), F32)] * 2,
        in_specs=[vmem, hbm, hbm, vmem],
        out_specs=[hbm, hbm],
        scratch_shapes=[
            pltpu.VMEM((n_tm - 1, pairs, days), F32),
            pltpu.VMEM((pairs, lag_pad, st_eof.shape[2]), F32),
            pltpu.VMEM((chunks, 2, 2 * depth, width), BF16),
            pltpu.VMEM((2, rows, 2 * depth), BF16),
            pltpu.VMEM((chunks, 2, rows, width), BF16),
            pltpu.VMEM((chunks, 2, rows, width), BF16),
            pltpu.VMEM((chunks, 2, rows, width), BF16),
            pltpu.VMEM((chunks, 2, 2 * days, width), BF16),
            pltpu.VMEM((chunks, 2, 2 * days, width), BF16),
            pltpu.VMEM((chunks, 2, rows, width), F32),
            pltpu.VMEM((3 * lat, width), F32),
            dma,
            dma((n_tm - 1,)),
            dma((n_tm - 1,)),
            dma((2, chunks)),
            dma((2, chunks)),
            dma((2, chunks)),
            dma((2, chunks)),
            dma((2, chunks)),
            dma((2, chunks)),
            dma((2, chunks)),
            dma((2, chunks)),
        ],
        compiler_params=pltpu.CompilerParams(
            collective_id=0, has_side_effects=True, vmem_limit_bytes=62 * 1024 * 1024
        ),
        name="reconstruct",
    )(pcs, st_eof, spatial_eof.reshape(2, depth, lon), land_sea)
    return vorticity.reshape(days, lat, lon), divergence.reshape(days, lat, lon)


def solution(mesh):
    return jax.shard_map(
        shards,
        mesh=mesh,
        in_specs=(P(None, "tm"), P(), P(None, "tm", "tile", None), P("tile", None)),
        out_specs=(P("tm", "tile", None), P("tm", "tile", None)),
        check_vma=False,
    )
```
